32 devices in a mesh: grp: 2 (over y), orient: 4 (over z), rows: 4 (over x, core).
Axes of the slice: x: 2, y: 2, z: 4, core: 2. Of those that a mesh axis runs over, the one named last changes fastest.
Arguments:
- micrograph: bfloat16 [1024, 512], P(('grp', 'rows')), parts along dimension 0, may hold values from -6 to 6
- bank: bfloat16 [20, 512, 512], P(None, 'rows'), may hold values from -0.01171875 to 0.01171875
- orient_index: int32 [16], P('orient'), may hold values from 0 to 19
- noise_power: float32 [1024, 512], P('grp'), parts along dimension 0, may hold values from 0.25 to 4
- defocus: float32 [2], P('grp'), parts along dimension 0, may hold values from 150 to 300
Outputs:
- peak: float32 [1024, 512], P(('grp', 'rows'), 'orient'), parts along dimension 0
- total: float32 [1024, 512], P(('grp', 'rows'), 'orient'), parts along dimension 0
- squares: float32 [1024, 512], P(('grp', 'rows'), 'orient'), parts along dimension 0
The draws below stay inside these ranges and needn't reach their ends.
There are 2 independent parts, one for each index of `grp`. The reference program is written for one: setup_inputs(seed, part) draws one part's arguments, and reference() takes and returns one part's arrays. A program takes and returns all parts, laid end to end along the dimension named above; an argument that names none is the same for every part. Nothing has to cross between parts.
All inputs are finite; a program needn't handle non-finite values.
Results may differ from the reference program's by a relative error of at most 0.0077.
Values may be sent and summed in bfloat16 or wider, within the bound.
A program may use at most 64 MiB of HBM per device.

```python
import math
import jax
import jax.numpy as jnp
from jax import lax

S = 512
MROWS = 512
COLS = 512
ORIENTS = 16
NPROJ = 20


def with_ends(drawn, rng, low, high):
    index_at = [jax.random.randint(jax.random.fold_in(rng, axis), (), 0, length) for axis, length in enumerate(drawn.shape)]
    main_axis = drawn.shape.index(max(drawn.shape))
    beside = index_at[:main_axis] + [(index_at[main_axis] + 1) % drawn.shape[main_axis]] + index_at[main_axis + 1:]
    return drawn.at[tuple(index_at)].set(low).at[tuple(beside)].set(high)


def block_scale(rng, extent, cuts, smallest, high):
    gain, own = 1.0, jax.random.fold_in(rng, 6)
    for dim, blocks in cuts:
        heights = jnp.exp(jax.random.uniform(jax.random.fold_in(own, dim), (blocks,), jnp.float32, smallest / len(cuts), high / len(cuts)))
        gain = gain * jnp.repeat(heights, extent[dim] // blocks).reshape([-1 if axis == dim else 1 for axis in range(len(extent))])
    return gain


def scatter_about(key, extent, deviation, most, cuts=(), dtype=jnp.bfloat16):
    loudness = block_scale(key, extent, cuts, -0.22, 0.18) if cuts else 1.0
    values = jax.random.normal(key, extent, jnp.float32) * deviation * loudness
    return jnp.minimum(jnp.maximum(values, -most), most).astype(dtype)


def setup_inputs(seed: int = 0, part: int = 0) -> dict:
    keys = jax.random.split(jax.random.key(seed), 6)
    part_splits = jax.random.split(jax.random.fold_in(keys[5], part), 6)
    micrograph = scatter_about(part_splits[0], (MROWS, COLS), 1.0, 6.0, ((0, 4),))
    bank = scatter_about(keys[1], (NPROJ, S, S), (S * S) ** -0.5, 0.01171875, ((1, 4),))
    orient_index = with_ends(jax.random.randint(keys[2], (ORIENTS,), 0, NPROJ), jax.random.fold_in(keys[2], 1), 0, NPROJ - 1).astype(jnp.int32)
    noise_power = jnp.clip(jnp.exp(jax.random.uniform(part_splits[3], (MROWS, COLS), jnp.float32, math.log(0.25), math.log(4.0))), 0.25, 4.0)
    defocus = jnp.clip(jax.random.uniform(part_splits[4], (1,), jnp.float32, 150.0, 300.0), 150.0, 300.0)
    return dict(micrograph=micrograph, bank=bank, orient_index=orient_index, noise_power=noise_power, defocus=defocus)


def tables(count, first, nrows, ncols):
    left = lax.iota(jnp.int32, nrows)[:, None] + first
    right = lax.iota(jnp.int32, ncols)[None, :]
    phase = (left * right % count).astype(jnp.float32) * (2.0 * math.pi / count)
    return (jnp.cos(phase).astype(jnp.bfloat16), jnp.sin(phase).astype(jnp.bfloat16))

def spectral_filter(row_ids, col_ids, nrows, ncols, defocus_value, noise):
    freq_y = ((row_ids + nrows // 2) % nrows - nrows // 2).astype(jnp.float32) / nrows
    freq_x = ((col_ids + ncols // 2) % ncols - ncols // 2).astype(jnp.float32) / ncols
    radius = freq_y[:, None] ** 2 + freq_x[None, :] ** 2
    chi = math.pi * defocus_value * radius
    return -(0.9975 * jnp.sin(chi) + 0.07 * jnp.cos(chi)) * lax.rsqrt(noise)

def mm(a, b):
    return jnp.dot(a, b, preferred_element_type=jnp.float32)

def reference(micrograph, bank, orient_index, noise_power, defocus):
    nrows, ncols = micrograph.shape
    side = bank.shape[1]
    lcos, lsin = tables(nrows, 0, nrows, nrows)
    ccos, csin = tables(ncols, 0, ncols, ncols)
    mic_re = mm(micrograph, ccos.T).astype(jnp.bfloat16)
    mic_im = (-mm(micrograph, csin.T)).astype(jnp.bfloat16)
    spec_re = mm(lcos, mic_re) + mm(lsin, mic_im)
    spec_im = mm(lcos, mic_im) - mm(lsin, mic_re)
    filt = spectral_filter(lax.iota(jnp.int32, nrows), lax.iota(jnp.int32, ncols), nrows, ncols, defocus[0], noise_power)
    scale = 1.0 / (nrows * ncols)
    tcos = ccos[:, :side].T
    tsin = csin[:, :side].T
    lcos_t = lcos[:, :side]
    lsin_t = lsin[:, :side]

    def step(carry, index):
        proj = lax.dynamic_index_in_dim(bank, index.astype(jnp.int32), 0, keepdims=False)
        tmp_re = mm(proj, tcos).astype(jnp.bfloat16)
        tmp_im = (-mm(proj, tsin)).astype(jnp.bfloat16)
        proj_re = mm(lcos_t, tmp_re) + mm(lsin_t, tmp_im)
        proj_im = mm(lcos_t, tmp_im) - mm(lsin_t, tmp_re)
        cross_re = (filt * (spec_re * proj_re + spec_im * proj_im)).astype(jnp.bfloat16)
        cross_im = (filt * (spec_im * proj_re - spec_re * proj_im)).astype(jnp.bfloat16)
        half_re = (mm(lcos, cross_re) - mm(lsin, cross_im)).astype(jnp.bfloat16)
        half_im = (mm(lcos, cross_im) + mm(lsin, cross_re)).astype(jnp.bfloat16)
        corr = (mm(half_re, ccos) - mm(half_im, csin)) * scale
        best, summed, squared = carry
        return ((jnp.maximum(best, corr), summed + corr, squared + corr * corr), None)
    start = (jnp.full((nrows, ncols), -jnp.inf, jnp.float32), jnp.zeros((nrows, ncols), jnp.float32), jnp.zeros((nrows, ncols), jnp.float32))
    (peak, total, squares), _ = lax.scan(step, start, orient_index)
    return (peak, total, squares)
```

```python
import functools
import math

import jax
import jax.numpy as jnp
import numpy as np
from jax import lax
from jax.experimental import pallas as pl
from jax.experimental.pallas import tpu as pltpu
from jax.sharding import PartitionSpec as P


def tables(count, nrows, ncols):
    left = lax.iota(jnp.int32, nrows)[:, None]
    right = lax.iota(jnp.int32, ncols)[None, :]
    phase = (left * right % count).astype(jnp.float32) * (2.0 * math.pi / count)
    return (jnp.cos(phase).astype(jnp.bfloat16), jnp.sin(phase).astype(jnp.bfloat16))


def spectral_filter(row_ids, col_ids, nrows, ncols, defocus_value, noise):
    freq_y = ((row_ids + nrows // 2) % nrows - nrows // 2).astype(jnp.float32) / nrows
    freq_x = ((col_ids + ncols // 2) % ncols - ncols // 2).astype(jnp.float32) / ncols
    radius = freq_y[:, None] ** 2 + freq_x[None, :] ** 2
    chi = math.pi * defocus_value * radius
    return -(0.9975 * jnp.sin(chi) + 0.07 * jnp.cos(chi)) * lax.rsqrt(noise)


def mm(a, b):
    return jnp.dot(a, b, preferred_element_type=jnp.float32)


def general(micrograph, bank, orient_index, noise_power, defocus):
    slab, ncols = micrograph.shape
    n_rows = lax.axis_size("rows")
    nrows = slab * n_rows
    row_pos = lax.axis_index("rows")
    lcos, lsin = tables(nrows, nrows, nrows)
    ccos, csin = tables(ncols, ncols, ncols)
    piece = lax.all_gather(micrograph, "rows", axis=0, tiled=True)
    part_re = mm(piece, ccos.T).astype(jnp.bfloat16)
    part_im = (-mm(piece, csin.T)).astype(jnp.bfloat16)
    new_re = mm(lcos, part_re) + mm(lsin, part_im)
    new_im = mm(lcos, part_im) - mm(lsin, part_re)
    chosen = jnp.take(bank, orient_index, axis=0)
    mine = lax.all_to_all(chosen, "rows", split_axis=0, concat_axis=1, tiled=True)
    filt = spectral_filter(
        lax.iota(jnp.int32, nrows),
        lax.iota(jnp.int32, ncols),
        nrows,
        ncols,
        defocus[0],
        noise_power,
    )
    scale = 1.0 / (nrows * ncols)
    tcos = ccos.T
    tsin = csin.T

    def correlate(carry, proj):
        tmp_re = mm(proj, tcos).astype(jnp.bfloat16)
        tmp_im = (-mm(proj, tsin)).astype(jnp.bfloat16)
        proj_re = mm(lcos, tmp_re) + mm(lsin, tmp_im)
        proj_im = mm(lcos, tmp_im) - mm(lsin, tmp_re)
        cross_re = (filt * (new_re * proj_re + new_im * proj_im)).astype(jnp.bfloat16)
        cross_im = (filt * (new_im * proj_re - new_re * proj_im)).astype(jnp.bfloat16)
        half_re = (mm(lcos, cross_re) - mm(lsin, cross_im)).astype(jnp.bfloat16)
        half_im = (mm(lcos, cross_im) + mm(lsin, cross_re)).astype(jnp.bfloat16)
        corr = (mm(half_re, ccos) - mm(half_im, csin)) * scale
        best_now, sum_now, square_now = carry
        return ((jnp.maximum(best_now, corr), sum_now + corr, square_now + corr * corr), None)

    start = (
        jnp.full((nrows, ncols), -jnp.inf, jnp.float32),
        jnp.zeros((nrows, ncols), jnp.float32),
        jnp.zeros((nrows, ncols), jnp.float32),
    )
    (best, summed, squared), _ = lax.scan(correlate, start, mine)
    width = ncols // lax.axis_size("orient")
    best = lax.pmax(best, ("orient", "rows"))
    summed, squared = lax.psum((summed, squared), ("orient", "rows"))
    first_col = lax.axis_index("orient") * width
    first_row = row_pos * slab

    def block(field):
        picked = lax.dynamic_slice_in_dim(field, first_row, slab, 0)
        return lax.dynamic_slice_in_dim(picked, first_col, width, 1)

    peak = block(best)
    total = block(summed)
    squares = block(squared)
    return (peak, total, squares)

MESH = pl.DeviceIdType.MESH


def wide_table(count):
    index = np.arange(count)
    phase = (index[:, None] * index[None, :] % count).astype(np.float32) * np.float32(2.0 * math.pi / count)
    cos = np.cos(phase)
    sin = np.sin(phase)
    return np.concatenate([sin, cos, -sin], axis=1).astype(jnp.bfloat16)


def dot(a, b):
    return jnp.dot(a, b, preferred_element_type=jnp.float32)


def kernel(n, m, size, defocus, mic, chosen, noise_hbm, table_hbm, peak, total, squares,
           noise, table, mics, projs, tmp, spec_re, spec_im, cross, half, stage, inbox,
           local_sem, mic_send, mic_recv, bank_send, bank_recv, out_send, out_recv):
    row = lax.axis_index("rows")
    col = lax.axis_index("orient")
    slab = size // n
    width = size // m
    me = row * m + col
    barrier = pltpu.get_barrier_semaphore()
    for a in range(n):
        for b in range(m):
            if a or b:
                peer = {"rows": lax.rem(row + a, n), "orient": lax.rem(col + b, m)}
                pl.semaphore_signal(barrier, inc=1, device_id=peer, device_id_type=MESH)
    table_copy = pltpu.make_async_copy(table_hbm, table, local_sem.at[0])
    noise_copy = pltpu.make_async_copy(noise_hbm, noise, local_sem.at[1])
    table_copy.start()
    noise_copy.start()
    pl.semaphore_wait(barrier, n * m - 1)

    order = sorted(range(1, n), key=lambda s: (s != n // 2, s))

    def mic_copy(peer, slot):
        return pltpu.make_async_remote_copy(
            src_ref=mic, dst_ref=mics.at[slot], send_sem=mic_send.at[peer], recv_sem=mic_recv.at[slot],
            device_id={"rows": peer}, device_id_type=MESH)

    def bank_copy(peer, slot):
        return pltpu.make_async_remote_copy(
            src_ref=chosen.at[peer], dst_ref=projs.at[slot], send_sem=bank_send.at[peer], recv_sem=bank_recv.at[slot],
            device_id={"rows": peer}, device_id_type=MESH)

    for s in order:
        mic_copy(lax.rem(row + s, n), row).start()
    for s in order:
        bank_copy(lax.rem(row + s, n), row).start()

    def row_dft(block, source):
        at = pl.multiple_of(source * slab, slab)
        both = dot(block, table[:, 0:2 * size]).astype(jnp.bfloat16)
        tmp[pl.ds(at, slab), :] = both[:, size:]
        tmp[pl.ds(pl.multiple_of(size + source * slab, slab), slab), :] = both[:, :size]

    table_copy.wait()
    row_dft(mic[...], row)
    noise_copy.wait()
    for s in order:
        source = lax.rem(row + n - s, n)
        mic_copy(source, source).wait_recv()
        row_dft(mics[source], source)

    def freq_angle(shape, dim):
        k = lax.broadcasted_iota(jnp.int32, shape, dim)
        f = jnp.where(k < size // 2, k, k - size).astype(jnp.float32) / size
        return math.pi * defocus[0] * f * f

    step = 256
    across = freq_angle((8, size), 1)
    sin_x = jnp.sin(across)[0:1]
    cos_x = jnp.cos(across)[0:1]
    left_x = -(0.9975 * cos_x - 0.07 * sin_x)
    right_x = -(0.9975 * sin_x + 0.07 * cos_x)
    down = freq_angle((size, 128), 0)
    sin_y = jnp.sin(down)[:, 0:1]
    cos_y = jnp.cos(down)[:, 0:1]
    for g in range(size // step):
        rows_g = slice(g * step, (g + 1) * step)
        filt = (sin_y[rows_g] * left_x + cos_y[rows_g] * right_x) * lax.rsqrt(noise[rows_g, :])
        spec_re[rows_g, :] = filt * dot(table[rows_g, size:], tmp[...])
        spec_im[rows_g, :] = filt * dot(table[rows_g, :2 * size], tmp[...])

    row_dft(chosen[row], row)
    for s in order:
        source = lax.rem(row + n - s, n)
        bank_copy(source, source).wait_recv()
        row_dft(projs[source], source)
    for g in range(size // step):
        rows_g = slice(g * step, (g + 1) * step)
        p_re = dot(table[rows_g, size:], tmp[...])
        p_im = dot(table[rows_g, :2 * size], tmp[...])
        s_re = spec_re[rows_g, :]
        s_im = spec_im[rows_g, :]
        cross[rows_g, :] = (s_re * p_re + s_im * p_im).astype(jnp.bfloat16)
        cross[size + g * step:size + (g + 1) * step, :] = (s_re * p_im - s_im * p_re).astype(jnp.bfloat16)

    def out_copy(a, b, slot):
        peer = a * m + b
        return pltpu.make_async_remote_copy(
            src_ref=stage.at[peer], dst_ref=inbox.at[slot], send_sem=out_send.at[peer], recv_sem=out_recv.at[slot],
            device_id={"rows": a, "orient": b}, device_id_type=MESH)

    scale = 1.0 / (size * size)
    pairs = n // 2
    for t in range(1, pairs + 1):
        g = lax.rem(row // 2 + t, pairs)
        at = pl.ds(pl.multiple_of(g * 2 * slab, 2 * slab), 2 * slab)
        half[:, :size] = dot(table[at, size:], cross[...]).astype(jnp.bfloat16)
        half[:, size:] = dot(table[at, :2 * size], cross[...]).astype(jnp.bfloat16)
        corr = (dot(half[:, :size], table[:, size:2 * size]) + dot(half[:, size:], table[:, 2 * size:])) * scale
        corr = corr.astype(jnp.bfloat16)
        for i in range(2):
            for b in range(m):
                stage[(g * 2 + i) * m + b] = corr[i * slab:(i + 1) * slab, b * width:(b + 1) * width]
        mate = lax.rem(row, 2)
        for i in range(2):
            a = g * 2 + lax.rem(mate + 1 + i, 2)
            for s in (m // 2, *(s for s in range(m) if s != m // 2)):
                if t == pairs and i == 1 and s == 0:
                    continue
                out_copy(a, lax.rem(col + s, m), me).start()

    best = summed = stage[me].astype(jnp.float32)
    squared = best * best
    for a in range(n):
        for b in range(m):
            if a or b:
                ra = lax.rem(row + n - a, n)
                rb = lax.rem(col + m - b, m)
                source = ra * m + rb
                out_copy(ra, rb, source).wait_recv()
                value = inbox[source].astype(jnp.float32)
                best = jnp.maximum(best, value)
                summed = summed + value
                squared = squared + value * value
    peak[...] = best
    total[...] = summed
    squares[...] = squared
    for s in order:
        peer = lax.rem(row + s, n)
        mic_copy(peer, row).wait_send()
        bank_copy(peer, row).wait_send()
    for a in range(n):
        for b in range(m):
            if a or b:
                out_copy(lax.rem(row + a, n), lax.rem(col + b, m), me).wait_send()


def local(micrograph, bank, orient_index, noise_power, defocus):
    slab, size = micrograph.shape
    n = lax.axis_size("rows")
    m = lax.axis_size("orient")
    fits = size == slab * n and n % 2 == 0 and slab % 128 == 0 and (size // m) % 128 == 0 and size % 256 == 0
    if not (fits and orient_index.shape[0] == n):
        return general(micrograph, bank, orient_index, noise_power, defocus)
    chosen = jnp.take(bank, orient_index, axis=0)
    table = jnp.asarray(wide_table(size))
    width = size // m
    out = jax.ShapeDtypeStruct((slab, width), jnp.float32)
    vmem = pl.BlockSpec(memory_space=pltpu.VMEM)
    hbm = pl.BlockSpec(memory_space=pl.ANY)
    bf16 = jnp.bfloat16
    dma = pltpu.SemaphoreType.DMA
    return pl.pallas_call(
        functools.partial(kernel, n, m, size),
        out_shape=(out, out, out),
        in_specs=[pl.BlockSpec(memory_space=pltpu.SMEM), vmem, vmem, hbm, hbm],
        out_specs=(vmem, vmem, vmem),
        scratch_shapes=[
            pltpu.VMEM((size, size), jnp.float32),
            pltpu.VMEM((size, 3 * size), bf16),
            pltpu.VMEM((n, slab, size), bf16),
            pltpu.VMEM((n, slab, size), bf16),
            pltpu.VMEM((2 * size, size), bf16),
            pltpu.VMEM((size, size), jnp.float32),
            pltpu.VMEM((size, size), jnp.float32),
            pltpu.VMEM((2 * size, size), bf16),
            pltpu.VMEM((2 * slab, 2 * size), bf16),
            pltpu.VMEM((n * m, slab, width), bf16),
            pltpu.VMEM((n * m, slab, width), bf16),
            dma((2,)), dma((n,)), dma((n,)), dma((n,)), dma((n,)), dma((n * m,)), dma((n * m,)),
        ],
        compiler_params=pltpu.CompilerParams(collective_id=0, has_side_effects=True, vmem_limit_bytes=48 * 1024 * 1024),
        name="correlate",
    )(defocus, micrograph, chosen, noise_power, table)


def solution(mesh):
    in_specs = (
        P(("grp", "rows"), None),
        P(None, "rows", None),
        P("orient"),
        P("grp", None),
        P("grp"),
    )
    out_specs = (
        P(("grp", "rows"), "orient"),
        P(("grp", "rows"), "orient"),
        P(("grp", "rows"), "orient"),
    )
    return jax.shard_map(local, mesh=mesh, in_specs=in_specs, out_specs=out_specs, check_vma=False)
```

```python
import functools
import math

import jax
import jax.numpy as jnp
import numpy as np
from jax import lax
from jax.experimental import pallas as pl
from jax.experimental.pallas import tpu as pltpu
from jax.sharding import PartitionSpec as P


def tables(count, nrows, ncols):
    left = lax.iota(jnp.int32, nrows)[:, None]
    right = lax.iota(jnp.int32, ncols)[None, :]
    phase = (left * right % count).astype(jnp.float32) * (2.0 * math.pi / count)
    return (jnp.cos(phase).astype(jnp.bfloat16), jnp.sin(phase).astype(jnp.bfloat16))


def spectral_filter(row_ids, col_ids, nrows, ncols, defocus_value, noise):
    freq_y = ((row_ids + nrows // 2) % nrows - nrows // 2).astype(jnp.float32) / nrows
    freq_x = ((col_ids + ncols // 2) % ncols - ncols // 2).astype(jnp.float32) / ncols
    radius = freq_y[:, None] ** 2 + freq_x[None, :] ** 2
    chi = math.pi * defocus_value * radius
    return -(0.9975 * jnp.sin(chi) + 0.07 * jnp.cos(chi)) * lax.rsqrt(noise)


def mm(a, b):
    return jnp.dot(a, b, preferred_element_type=jnp.float32)


def general(micrograph, bank, orient_index, noise_power, defocus):
    slab, ncols = micrograph.shape
    n_rows = lax.axis_size("rows")
    nrows = slab * n_rows
    row_pos = lax.axis_index("rows")
    lcos, lsin = tables(nrows, nrows, nrows)
    ccos, csin = tables(ncols, ncols, ncols)
    piece = lax.all_gather(micrograph, "rows", axis=0, tiled=True)
    part_re = mm(piece, ccos.T).astype(jnp.bfloat16)
    part_im = (-mm(piece, csin.T)).astype(jnp.bfloat16)
    new_re = mm(lcos, part_re) + mm(lsin, part_im)
    new_im = mm(lcos, part_im) - mm(lsin, part_re)
    chosen = jnp.take(bank, orient_index, axis=0)
    mine = lax.all_to_all(chosen, "rows", split_axis=0, concat_axis=1, tiled=True)
    filt = spectral_filter(
        lax.iota(jnp.int32, nrows),
        lax.iota(jnp.int32, ncols),
        nrows,
        ncols,
        defocus[0],
        noise_power,
    )
    scale = 1.0 / (nrows * ncols)
    tcos = ccos.T
    tsin = csin.T

    def correlate(carry, proj):
        tmp_re = mm(proj, tcos).astype(jnp.bfloat16)
        tmp_im = (-mm(proj, tsin)).astype(jnp.bfloat16)
        proj_re = mm(lcos, tmp_re) + mm(lsin, tmp_im)
        proj_im = mm(lcos, tmp_im) - mm(lsin, tmp_re)
        cross_re = (filt * (new_re * proj_re + new_im * proj_im)).astype(jnp.bfloat16)
        cross_im = (filt * (new_im * proj_re - new_re * proj_im)).astype(jnp.bfloat16)
        half_re = (mm(lcos, cross_re) - mm(lsin, cross_im)).astype(jnp.bfloat16)
        half_im = (mm(lcos, cross_im) + mm(lsin, cross_re)).astype(jnp.bfloat16)
        corr = (mm(half_re, ccos) - mm(half_im, csin)) * scale
        best_now, sum_now, square_now = carry
        return ((jnp.maximum(best_now, corr), sum_now + corr, square_now + corr * corr), None)

    start = (
        jnp.full((nrows, ncols), -jnp.inf, jnp.float32),
        jnp.zeros((nrows, ncols), jnp.float32),
        jnp.zeros((nrows, ncols), jnp.float32),
    )
    (best, summed, squared), _ = lax.scan(correlate, start, mine)
    width = ncols // lax.axis_size("orient")
    best = lax.pmax(best, ("orient", "rows"))
    summed, squared = lax.psum((summed, squared), ("orient", "rows"))
    first_col = lax.axis_index("orient") * width
    first_row = row_pos * slab

    def block(field):
        picked = lax.dynamic_slice_in_dim(field, first_row, slab, 0)
        return lax.dynamic_slice_in_dim(picked, first_col, width, 1)

    peak = block(best)
    total = block(summed)
    squares = block(squared)
    return (peak, total, squares)

MESH = pl.DeviceIdType.MESH


def wide_table(count):
    index = np.arange(count)
    phase = (index[:, None] * index[None, :] % count).astype(np.float32) * np.float32(2.0 * math.pi / count)
    cos = np.cos(phase)
    sin = np.sin(phase)
    return np.concatenate([sin, cos, -sin], axis=1).astype(jnp.bfloat16)


def dot(a, b):
    return jnp.dot(a, b, preferred_element_type=jnp.float32)


def kernel(n, m, size, defocus, index, mic_hbm, bank_hbm, noise_hbm, table_hbm, peak, total, squares,
           bank, chosen, mic, noise, table, mics, halves, beside, tmp_mic, tmp, proj_re, proj_im, cross, half, stage, inbox,
           local_sem, near, out_send, out_recv):
    row = lax.axis_index("rows")
    col = lax.axis_index("orient")
    slab = size // n
    width = size // m
    me = row * m + col
    grp = lax.axis_index("grp")
    over = row + 2 - 4 * (row // 2)
    mate = row + 1 - 2 * lax.rem(row, 2)
    corner = mate + 2 - 4 * (mate // 2)
    piece = slab // 2
    barrier = pltpu.get_barrier_semaphore()
    for a in range(n):
        for b in range(m):
            if a or b:
                peer = {"rows": lax.rem(row + a, n), "orient": lax.rem(col + b, m)}
                pl.semaphore_signal(barrier, inc=1, device_id=peer, device_id_type=MESH)
    pl.semaphore_signal(barrier, inc=1, device_id={"grp": 1 - grp}, device_id_type=MESH)
    mic_in = pltpu.make_async_copy(mic_hbm, mic, local_sem.at[0])
    table_in = pltpu.make_async_copy(table_hbm, table, local_sem.at[1])
    noise_in = pltpu.make_async_copy(noise_hbm, noise, local_sem.at[2])
    bank_in = pltpu.make_async_copy(bank_hbm, bank, local_sem.at[3])
    bank_in.start()
    mic_in.start()
    table_in.start()
    noise_in.start()
    bank_in.wait()
    for d in range(n):
        chosen[d] = bank[index[d]]
    mic_in.wait()
    pl.semaphore_wait(barrier, n * m)

    def remote(src, dst, sems, at, to):
        return pltpu.make_async_remote_copy(
            src_ref=src, dst_ref=dst, send_sem=sems.at[0, at], recv_sem=sems.at[1, at],
            device_id=to, device_id_type=MESH)

    bank_over = remote(chosen.at[over, pl.ds(grp * piece, piece)], halves.at[0, grp], near, 0, {"rows": over})
    bank_corner = remote(chosen.at[corner, pl.ds(grp * piece, piece)], halves.at[1, grp], near, 1, {"rows": corner})
    bank_mate = remote(chosen.at[mate], beside.at[0], near, 2, {"rows": mate})
    mic_over = remote(mic, mics.at[0], near, 3, {"rows": over})
    mic_mate = remote(mic, mics.at[1], near, 4, {"rows": mate})
    mic_pass = remote(mics.at[0], mics.at[2], near, 5, {"rows": mate})
    pass_over = remote(halves.at[0, grp], halves.at[0, grp], near, 6, {"grp": 1 - grp})
    pass_corner = remote(halves.at[1, grp], halves.at[1, grp], near, 7, {"grp": 1 - grp})
    bank_over.start()
    bank_corner.start()
    mic_over.start()
    mic_mate.start()
    bank_mate.start()

    def row_dft(into, block, source):
        at = pl.multiple_of(source * slab, slab)
        both = dot(block, table[:, 0:2 * size]).astype(jnp.bfloat16)
        into[pl.ds(at, slab), :] = both[:, size:]
        into[pl.ds(pl.multiple_of(size + source * slab, slab), slab), :] = both[:, :size]

    table_in.wait()
    row_dft(tmp_mic, mic[...], row)
    row_dft(tmp, chosen[row], row)
    bank_over.wait_recv()
    pass_over.start()
    mic_mate.wait_recv()
    row_dft(tmp_mic, mics[1], mate)
    bank_corner.wait_recv()
    pass_corner.start()
    bank_mate.wait_recv()
    row_dft(tmp, beside[0], mate)
    noise_in.wait()

    def freq_angle(shape, dim):
        k = lax.broadcasted_iota(jnp.int32, shape, dim)
        f = jnp.where(k < size // 2, k, k - size).astype(jnp.float32) / size
        return math.pi * defocus[0] * f * f

    step = 256
    across = freq_angle((8, size), 1)
    sin_x = jnp.sin(across)[0:1]
    cos_x = jnp.cos(across)[0:1]
    left_x = -(0.9975 * cos_x - 0.07 * sin_x)
    right_x = -(0.9975 * sin_x + 0.07 * cos_x)
    down = freq_angle((size, 128), 0)
    sin_y = jnp.sin(down)[:, 0:1]
    cos_y = jnp.cos(down)[:, 0:1]
    for g in range(size // step):
        rows_g = slice(g * step, (g + 1) * step)
        noise[rows_g, :] = (sin_y[rows_g] * left_x + cos_y[rows_g] * right_x) * lax.rsqrt(noise[rows_g, :])
    pass_over.wait_recv()
    row_dft(tmp, halves[0].reshape(slab, size), over)
    mic_over.wait_recv()
    mic_pass.start()
    pass_corner.wait_recv()
    row_dft(tmp, halves[1].reshape(slab, size), corner)
    row_dft(tmp_mic, mics[0], over)
    for g in range(size // step):
        rows_g = slice(g * step, (g + 1) * step)
        proj_re[rows_g, :] = noise[rows_g, :] * dot(table[rows_g, size:], tmp[...])
        proj_im[rows_g, :] = noise[rows_g, :] * dot(table[rows_g, :2 * size], tmp[...])
    mic_pass.wait_recv()
    row_dft(tmp_mic, mics[2], corner)
    for g in range(size // step):
        rows_g = slice(g * step, (g + 1) * step)
        s_re = dot(table[rows_g, size:], tmp_mic[...])
        s_im = dot(table[rows_g, :2 * size], tmp_mic[...])
        p_re = proj_re[rows_g, :]
        p_im = proj_im[rows_g, :]
        cross[rows_g, :] = (s_re * p_re + s_im * p_im).astype(jnp.bfloat16)
        cross[size + g * step:size + (g + 1) * step, :] = (s_re * p_im - s_im * p_re).astype(jnp.bfloat16)

    def out_copy(a, b, slot):
        peer = a * m + b
        return pltpu.make_async_remote_copy(
            src_ref=stage.at[peer], dst_ref=inbox.at[slot], send_sem=out_send.at[peer], recv_sem=out_recv.at[slot],
            device_id={"rows": a, "orient": b}, device_id_type=MESH)

    scale = 1.0 / (size * size)
    pairs = n // 2
    for t in range(1, pairs + 1):
        g = lax.rem(row // 2 + t, pairs)
        at = pl.ds(pl.multiple_of(g * 2 * slab, 2 * slab), 2 * slab)
        half[:, :size] = dot(table[at, size:], cross[...]).astype(jnp.bfloat16)
        half[:, size:] = dot(table[at, :2 * size], cross[...]).astype(jnp.bfloat16)
        corr = (dot(half[:, :size], table[:, size:2 * size]) + dot(half[:, size:], table[:, 2 * size:])) * scale
        corr = corr.astype(jnp.bfloat16)
        for i in range(2):
            for b in range(m):
                stage[(g * 2 + i) * m + b] = corr[i * slab:(i + 1) * slab, b * width:(b + 1) * width]
        for i in range(2):
            a = g * 2 + lax.rem(row + 1 + i, 2)
            for s in (m // 2, *(s for s in range(m) if s != m // 2)):
                if t == pairs and i == 1 and s == 0:
                    continue
                out_copy(a, lax.rem(col + s, m), me).start()

    best = summed = stage[me].astype(jnp.float32)
    squared = best * best
    for a in range(n):
        for b in range(m):
            if a or b:
                ra = lax.rem(row + n - a, n)
                rb = lax.rem(col + m - b, m)
                source = ra * m + rb
                out_copy(ra, rb, source).wait_recv()
                value = inbox[source].astype(jnp.float32)
                best = jnp.maximum(best, value)
                summed = summed + value
                squared = squared + value * value
    peak[...] = best
    total[...] = summed
    squares[...] = squared
    for copy in (bank_over, bank_corner, bank_mate, mic_over, mic_mate, mic_pass, pass_over, pass_corner):
        copy.wait_send()
    for a in range(n):
        for b in range(m):
            if a or b:
                out_copy(lax.rem(row + a, n), lax.rem(col + b, m), me).wait_send()


def write_out(peak_in, total_in, squares_in, peak, total, squares):
    peak[...] = peak_in[...]
    total[...] = total_in[...]
    squares[...] = squares_in[...]


def local(micrograph, bank, orient_index, noise_power, defocus):
    slab, size = micrograph.shape
    n = lax.axis_size("rows")
    m = lax.axis_size("orient")
    fits = size == slab * n and n == 4 and lax.axis_size("grp") == 2 and slab % 128 == 0 and (size // m) % 128 == 0 and size % 256 == 0
    if not (fits and orient_index.shape[0] == n and bank.shape[0] <= 64):
        return general(micrograph, bank, orient_index, noise_power, defocus)
    table = jnp.asarray(wide_table(size))
    width = size // m
    out = jax.ShapeDtypeStruct((slab, width), jnp.float32)
    vmem = pl.BlockSpec(memory_space=pltpu.VMEM)
    hbm = pl.BlockSpec(memory_space=pl.ANY)
    smem = pl.BlockSpec(memory_space=pltpu.SMEM)
    bf16 = jnp.bfloat16
    dma = pltpu.SemaphoreType.DMA
    maps = pl.pallas_call(
        functools.partial(kernel, n, m, size),
        out_shape=(out, out, out),
        in_specs=[smem, smem, hbm, hbm, hbm, hbm],
        out_specs=(vmem, vmem, vmem),
        scratch_shapes=[
            pltpu.VMEM(bank.shape, bf16),
            pltpu.VMEM((n, slab, size), bf16),
            pltpu.VMEM((slab, size), bf16),
            pltpu.VMEM((size, size), jnp.float32),
            pltpu.VMEM((size, 3 * size), bf16),
            pltpu.VMEM((3, slab, size), bf16),
            pltpu.VMEM((2, 2, slab // 2, size), bf16),
            pltpu.VMEM((1, slab, size), bf16),
            pltpu.VMEM((2 * size, size), bf16),
            pltpu.VMEM((2 * size, size), bf16),
            pltpu.VMEM((size, size), jnp.float32),
            pltpu.VMEM((size, size), jnp.float32),
            pltpu.VMEM((2 * size, size), bf16),
            pltpu.VMEM((2 * slab, 2 * size), bf16),
            pltpu.VMEM((n * m, slab, width), bf16),
            pltpu.VMEM((n * m, slab, width), bf16),
            dma((4,)), dma((2, 8)), dma((n * m,)), dma((n * m,)),
        ],
        compiler_params=pltpu.CompilerParams(collective_id=0, has_side_effects=True, vmem_limit_bytes=60 * 1024 * 1024),
        name="correlate",
    )(defocus, orient_index, micrograph, bank, noise_power, table)
    return pl.pallas_call(
        write_out,
        out_shape=(out, out, out),
        in_specs=[vmem] * 3,
        out_specs=(vmem, vmem, vmem),
        name="write_out",
    )(*maps)


def solution(mesh):
    in_specs = (
        P(("grp", "rows"), None),
        P(None, "rows", None),
        P("orient"),
        P("grp", None),
        P("grp"),
    )
    out_specs = (
        P(("grp", "rows"), "orient"),
        P(("grp", "rows"), "orient"),
        P(("grp", "rows"), "orient"),
    )
    return jax.shard_map(local, mesh=mesh, in_specs=in_specs, out_specs=out_specs, check_vma=False)
```

```python
import functools
import math

import jax
import jax.numpy as jnp
import numpy as np
from jax import lax
from jax.experimental import pallas as pl
from jax.experimental.pallas import tpu as pltpu
from jax.sharding import PartitionSpec as P


def tables(count, nrows, ncols):
    left = lax.iota(jnp.int32, nrows)[:, None]
    right = lax.iota(jnp.int32, ncols)[None, :]
    phase = (left * right % count).astype(jnp.float32) * (2.0 * math.pi / count)
    return (jnp.cos(phase).astype(jnp.bfloat16), jnp.sin(phase).astype(jnp.bfloat16))


def spectral_filter(row_ids, col_ids, nrows, ncols, defocus_value, noise):
    freq_y = ((row_ids + nrows // 2) % nrows - nrows // 2).astype(jnp.float32) / nrows
    freq_x = ((col_ids + ncols // 2) % ncols - ncols // 2).astype(jnp.float32) / ncols
    radius = freq_y[:, None] ** 2 + freq_x[None, :] ** 2
    chi = math.pi * defocus_value * radius
    return -(0.9975 * jnp.sin(chi) + 0.07 * jnp.cos(chi)) * lax.rsqrt(noise)


def mm(a, b):
    return jnp.dot(a, b, preferred_element_type=jnp.float32)


def general(micrograph, bank, orient_index, noise_power, defocus):
    slab, ncols = micrograph.shape
    n_rows = lax.axis_size("rows")
    nrows = slab * n_rows
    row_pos = lax.axis_index("rows")
    lcos, lsin = tables(nrows, nrows, nrows)
    ccos, csin = tables(ncols, ncols, ncols)
    piece = lax.all_gather(micrograph, "rows", axis=0, tiled=True)
    part_re = mm(piece, ccos.T).astype(jnp.bfloat16)
    part_im = (-mm(piece, csin.T)).astype(jnp.bfloat16)
    new_re = mm(lcos, part_re) + mm(lsin, part_im)
    new_im = mm(lcos, part_im) - mm(lsin, part_re)
    chosen = jnp.take(bank, orient_index, axis=0)
    mine = lax.all_to_all(chosen, "rows", split_axis=0, concat_axis=1, tiled=True)
    filt = spectral_filter(
        lax.iota(jnp.int32, nrows),
        lax.iota(jnp.int32, ncols),
        nrows,
        ncols,
        defocus[0],
        noise_power,
    )
    scale = 1.0 / (nrows * ncols)
    tcos = ccos.T
    tsin = csin.T

    def correlate(carry, proj):
        tmp_re = mm(proj, tcos).astype(jnp.bfloat16)
        tmp_im = (-mm(proj, tsin)).astype(jnp.bfloat16)
        proj_re = mm(lcos, tmp_re) + mm(lsin, tmp_im)
        proj_im = mm(lcos, tmp_im) - mm(lsin, tmp_re)
        cross_re = (filt * (new_re * proj_re + new_im * proj_im)).astype(jnp.bfloat16)
        cross_im = (filt * (new_im * proj_re - new_re * proj_im)).astype(jnp.bfloat16)
        half_re = (mm(lcos, cross_re) - mm(lsin, cross_im)).astype(jnp.bfloat16)
        half_im = (mm(lcos, cross_im) + mm(lsin, cross_re)).astype(jnp.bfloat16)
        corr = (mm(half_re, ccos) - mm(half_im, csin)) * scale
        best_now, sum_now, square_now = carry
        return ((jnp.maximum(best_now, corr), sum_now + corr, square_now + corr * corr), None)

    start = (
        jnp.full((nrows, ncols), -jnp.inf, jnp.float32),
        jnp.zeros((nrows, ncols), jnp.float32),
        jnp.zeros((nrows, ncols), jnp.float32),
    )
    (best, summed, squared), _ = lax.scan(correlate, start, mine)
    width = ncols // lax.axis_size("orient")
    best = lax.pmax(best, ("orient", "rows"))
    summed, squared = lax.psum((summed, squared), ("orient", "rows"))
    first_col = lax.axis_index("orient") * width
    first_row = row_pos * slab

    def block(field):
        picked = lax.dynamic_slice_in_dim(field, first_row, slab, 0)
        return lax.dynamic_slice_in_dim(picked, first_col, width, 1)

    peak = block(best)
    total = block(summed)
    squares = block(squared)
    return (peak, total, squares)

MESH = pl.DeviceIdType.MESH


def wide_table(count):
    index = np.arange(count)
    phase = (index[:, None] * index[None, :] % count).astype(np.float32) * np.float32(2.0 * math.pi / count)
    cos = np.cos(phase)
    sin = np.sin(phase)
    return np.concatenate([sin, cos, -sin], axis=1).astype(jnp.bfloat16)


def dot(a, b):
    return jnp.dot(a, b, preferred_element_type=jnp.float32)


def kernel(n, m, size, defocus, index, mic_hbm, bank_hbm, noise_hbm, table_hbm, peak, total, squares,
           bank, chosen, mic, noise, table, mics, halves, beside, tmp_mic, tmp, proj_re, proj_im, cross, half, stage, inbox, part,
           local_sem, near, out_send, out_recv):
    row = lax.axis_index("rows")
    col = lax.axis_index("orient")
    slab = size // n
    width = size // m
    me = row * 2 + lax.rem(col, 2)
    grp = lax.axis_index("grp")
    over = row + 2 - 4 * (row // 2)
    mate = row + 1 - 2 * lax.rem(row, 2)
    corner = mate + 2 - 4 * (mate // 2)
    piece = slab // 2
    barrier = pltpu.get_barrier_semaphore()
    low = 2 * (col // 2)
    far = 2 - low
    for a in range(n):
        for b in range(2):
            if a or b:
                peer = {"rows": lax.rem(row + a, n), "orient": low + lax.rem(col + b, 2)}
                pl.semaphore_signal(barrier, inc=1, device_id=peer, device_id_type=MESH)
    twin = {"orient": far + lax.rem(col, 2)}
    pl.semaphore_signal(barrier, inc=1, device_id=twin, device_id_type=MESH)
    pl.semaphore_signal(barrier, inc=1, device_id={"grp": 1 - grp}, device_id_type=MESH)
    mic_in = pltpu.make_async_copy(mic_hbm, mic, local_sem.at[0])
    table_in = pltpu.make_async_copy(table_hbm, table, local_sem.at[1])
    noise_in = pltpu.make_async_copy(noise_hbm, noise, local_sem.at[2])
    bank_in = pltpu.make_async_copy(bank_hbm, bank, local_sem.at[3])
    bank_in.start()
    mic_in.start()
    table_in.start()
    noise_in.start()
    bank_in.wait()
    for d in range(n):
        chosen[d] = bank[index[d]]
    mic_in.wait()
    pl.semaphore_wait(barrier, 2 * n + 1)

    def remote(src, dst, sems, at, to):
        return pltpu.make_async_remote_copy(
            src_ref=src, dst_ref=dst, send_sem=sems.at[0, at], recv_sem=sems.at[1, at],
            device_id=to, device_id_type=MESH)

    bank_over = remote(chosen.at[over, pl.ds(grp * piece, piece)], halves.at[0, grp], near, 0, {"rows": over})
    bank_corner = remote(chosen.at[corner, pl.ds(grp * piece, piece)], halves.at[1, grp], near, 1, {"rows": corner})
    bank_mate = remote(chosen.at[mate], beside.at[0], near, 2, {"rows": mate})
    mic_over = remote(mic, mics.at[0], near, 3, {"rows": over})
    mic_mate = remote(mic, mics.at[1], near, 4, {"rows": mate})
    mic_pass = remote(mics.at[0], mics.at[2], near, 5, {"rows": mate})
    pass_over = remote(halves.at[0, grp], halves.at[0, grp], near, 6, {"grp": 1 - grp})
    pass_corner = remote(halves.at[1, grp], halves.at[1, grp], near, 7, {"grp": 1 - grp})
    bank_over.start()
    bank_corner.start()
    mic_over.start()
    mic_mate.start()
    bank_mate.start()

    def row_dft(into, block, source):
        at = pl.multiple_of(source * slab, slab)
        both = dot(block, table[:, 0:2 * size]).astype(jnp.bfloat16)
        into[pl.ds(at, slab), :] = both[:, size:]
        into[pl.ds(pl.multiple_of(size + source * slab, slab), slab), :] = both[:, :size]

    table_in.wait()
    row_dft(tmp_mic, mic[...], row)
    row_dft(tmp, chosen[row], row)
    bank_over.wait_recv()
    pass_over.start()
    mic_mate.wait_recv()
    row_dft(tmp_mic, mics[1], mate)
    bank_corner.wait_recv()
    pass_corner.start()
    bank_mate.wait_recv()
    row_dft(tmp, beside[0], mate)
    noise_in.wait()

    def freq_angle(shape, dim):
        k = lax.broadcasted_iota(jnp.int32, shape, dim)
        f = jnp.where(k < size // 2, k, k - size).astype(jnp.float32) / size
        return math.pi * defocus[0] * f * f

    step = 256
    across = freq_angle((8, size), 1)
    sin_x = jnp.sin(across)[0:1]
    cos_x = jnp.cos(across)[0:1]
    left_x = -(0.9975 * cos_x - 0.07 * sin_x)
    right_x = -(0.9975 * sin_x + 0.07 * cos_x)
    down = freq_angle((size, 128), 0)
    sin_y = jnp.sin(down)[:, 0:1]
    cos_y = jnp.cos(down)[:, 0:1]
    for g in range(size // step):
        rows_g = slice(g * step, (g + 1) * step)
        noise[rows_g, :] = (sin_y[rows_g] * left_x + cos_y[rows_g] * right_x) * lax.rsqrt(noise[rows_g, :])
    pass_over.wait_recv()
    row_dft(tmp, halves[0].reshape(slab, size), over)
    mic_over.wait_recv()
    mic_pass.start()
    pass_corner.wait_recv()
    row_dft(tmp, halves[1].reshape(slab, size), corner)
    row_dft(tmp_mic, mics[0], over)
    for g in range(size // step):
        rows_g = slice(g * step, (g + 1) * step)
        proj_re[rows_g, :] = noise[rows_g, :] * dot(table[rows_g, size:], tmp[...])
        proj_im[rows_g, :] = noise[rows_g, :] * dot(table[rows_g, :2 * size], tmp[...])
    mic_pass.wait_recv()
    row_dft(tmp_mic, mics[2], corner)
    for g in range(size // step):
        rows_g = slice(g * step, (g + 1) * step)
        s_re = dot(table[rows_g, size:], tmp_mic[...])
        s_im = dot(table[rows_g, :2 * size], tmp_mic[...])
        p_re = proj_re[rows_g, :]
        p_im = proj_im[rows_g, :]
        cross[rows_g, :] = (s_re * p_re + s_im * p_im).astype(jnp.bfloat16)
        cross[size + g * step:size + (g + 1) * step, :] = (s_re * p_im - s_im * p_re).astype(jnp.bfloat16)

    def out_copy(kind, a, b, slot):
        peer = a * 2 + b
        return pltpu.make_async_remote_copy(
            src_ref=stage.at[kind, peer], dst_ref=inbox.at[kind, slot],
            send_sem=out_send.at[kind, peer], recv_sem=out_recv.at[kind, slot],
            device_id={"rows": a, "orient": low + b}, device_id_type=MESH)

    scale = 1.0 / (size * size)
    pairs = n // 2
    side = lax.rem(col, 2)

    def send_blocks(kind, t):
        g = lax.rem(row // 2 + t, pairs)
        begin = (far if kind == 0 else low) * width
        cos_at = pl.ds(pl.multiple_of(size + begin, 2 * width), 2 * width)
        sin_at = pl.ds(pl.multiple_of(2 * size + begin, 2 * width), 2 * width)
        corr = (dot(half[t - 1, :, :size], table[:, cos_at]) + dot(half[t - 1, :, size:], table[:, sin_at])) * scale
        corr = corr.astype(jnp.bfloat16)
        for i in range(2):
            for b in range(2):
                stage[kind, (g * 2 + i) * 2 + b] = corr[i * slab:(i + 1) * slab, b * width:(b + 1) * width]
        for i in range(2):
            a = g * 2 + lax.rem(row + 1 + i, 2)
            for s in (1, 0):
                if t == pairs and i == 1 and s == 0:
                    continue
                out_copy(kind, a, lax.rem(side + s, 2), me).start()

    for t in range(1, pairs + 1):
        at = pl.ds(pl.multiple_of(lax.rem(row // 2 + t, pairs) * 2 * slab, 2 * slab), 2 * slab)
        half[t - 1, :, :size] = dot(table[at, size:], cross[...]).astype(jnp.bfloat16)
        half[t - 1, :, size:] = dot(table[at, :2 * size], cross[...]).astype(jnp.bfloat16)
        send_blocks(0, t)
    for t in range(1, pairs + 1):
        send_blocks(1, t)

    def combine(kind):
        best = summed = stage[kind, me].astype(jnp.float32)
        squared = best * best
        for a in range(n):
            for b in range(2):
                if a or b:
                    ra = lax.rem(row + n - a, n)
                    rb = lax.rem(side + b, 2)
                    source = ra * 2 + rb
                    out_copy(kind, ra, rb, source).wait_recv()
                    value = inbox[kind, source].astype(jnp.float32)
                    best = jnp.maximum(best, value)
                    summed = summed + value
                    squared = squared + value * value
        return best, summed, squared

    best, summed, squared = combine(0)
    part[0, 0] = best.astype(jnp.bfloat16)
    part[0, 1] = summed.astype(jnp.bfloat16)
    part[0, 2] = squared.astype(jnp.bfloat16)
    part_copy = remote(part.at[0], part.at[1], near, 8, twin)
    part_copy.start()
    best, summed, squared = combine(1)
    part_copy.wait_recv()
    best = jnp.maximum(best, part[1, 0].astype(jnp.float32))
    summed = summed + part[1, 1].astype(jnp.float32)
    squared = squared + part[1, 2].astype(jnp.float32)
    peak[...] = best
    total[...] = summed
    squares[...] = squared
    for copy in (bank_over, bank_corner, bank_mate, mic_over, mic_mate, mic_pass, pass_over, pass_corner):
        copy.wait_send()
    part_copy.wait_send()
    for kind in range(2):
        for a in range(n):
            for b in range(2):
                if a or b:
                    out_copy(kind, lax.rem(row + a, n), lax.rem(side + b, 2), me).wait_send()


def write_out(peak_in, total_in, squares_in, peak, total, squares):
    peak[...] = peak_in[...]
    total[...] = total_in[...]
    squares[...] = squares_in[...]


def local(micrograph, bank, orient_index, noise_power, defocus):
    slab, size = micrograph.shape
    n = lax.axis_size("rows")
    m = lax.axis_size("orient")
    fits = size == slab * n and n == 4 and m == 4 and lax.axis_size("grp") == 2 and slab % 128 == 0 and (size // m) % 128 == 0 and size % 256 == 0
    if not (fits and orient_index.shape[0] == n and bank.shape[0] <= 64):
        return general(micrograph, bank, orient_index, noise_power, defocus)
    table = jnp.asarray(wide_table(size))
    width = size // m
    out = jax.ShapeDtypeStruct((slab, width), jnp.float32)
    vmem = pl.BlockSpec(memory_space=pltpu.VMEM)
    hbm = pl.BlockSpec(memory_space=pl.ANY)
    smem = pl.BlockSpec(memory_space=pltpu.SMEM)
    bf16 = jnp.bfloat16
    dma = pltpu.SemaphoreType.DMA
    maps = pl.pallas_call(
        functools.partial(kernel, n, m, size),
        out_shape=(out, out, out),
        in_specs=[smem, smem, hbm, hbm, hbm, hbm],
        out_specs=(vmem, vmem, vmem),
        scratch_shapes=[
            pltpu.VMEM(bank.shape, bf16),
            pltpu.VMEM((n, slab, size), bf16),
            pltpu.VMEM((slab, size), bf16),
            pltpu.VMEM((size, size), jnp.float32),
            pltpu.VMEM((size, 3 * size), bf16),
            pltpu.VMEM((3, slab, size), bf16),
            pltpu.VMEM((2, 2, slab // 2, size), bf16),
            pltpu.VMEM((1, slab, size), bf16),
            pltpu.VMEM((2 * size, size), bf16),
            pltpu.VMEM((2 * size, size), bf16),
            pltpu.VMEM((size, size), jnp.float32),
            pltpu.VMEM((size, size), jnp.float32),
            pltpu.VMEM((2 * size, size), bf16),
            pltpu.VMEM((n // 2, 2 * slab, 2 * size), bf16),
            pltpu.VMEM((2, 2 * n, slab, width), bf16),
            pltpu.VMEM((2, 2 * n, slab, width), bf16),
            pltpu.VMEM((2, 3, slab, width), bf16),
            dma((4,)), dma((2, 9)), dma((2, 2 * n)), dma((2, 2 * n)),
        ],
        compiler_params=pltpu.CompilerParams(collective_id=0, has_side_effects=True, vmem_limit_bytes=60 * 1024 * 1024),
        name="correlate",
    )(defocus, orient_index, micrograph, bank, noise_power, table)
    return pl.pallas_call(
        write_out,
        out_shape=(out, out, out),
        in_specs=[vmem] * 3,
        out_specs=(vmem, vmem, vmem),
        name="write_out",
    )(*maps)


def solution(mesh):
    in_specs = (
        P(("grp", "rows"), None),
        P(None, "rows", None),
        P("orient"),
        P("grp", None),
        P("grp"),
    )
    out_specs = (
        P(("grp", "rows"), "orient"),
        P(("grp", "rows"), "orient"),
        P(("grp", "rows"), "orient"),
    )
    return jax.shard_map(local, mesh=mesh, in_specs=in_specs, out_specs=out_specs, check_vma=False)
```

```python
import functools
import math

import jax
import jax.numpy as jnp
import numpy as np
from jax import lax
from jax.experimental import pallas as pl
from jax.experimental.pallas import tpu as pltpu
from jax.sharding import PartitionSpec as P


def tables(count, nrows, ncols):
    left = lax.iota(jnp.int32, nrows)[:, None]
    right = lax.iota(jnp.int32, ncols)[None, :]
    phase = (left * right % count).astype(jnp.float32) * (2.0 * math.pi / count)
    return (jnp.cos(phase).astype(jnp.bfloat16), jnp.sin(phase).astype(jnp.bfloat16))


def spectral_filter(row_ids, col_ids, nrows, ncols, defocus_value, noise):
    freq_y = ((row_ids + nrows // 2) % nrows - nrows // 2).astype(jnp.float32) / nrows
    freq_x = ((col_ids + ncols // 2) % ncols - ncols // 2).astype(jnp.float32) / ncols
    radius = freq_y[:, None] ** 2 + freq_x[None, :] ** 2
    chi = math.pi * defocus_value * radius
    return -(0.9975 * jnp.sin(chi) + 0.07 * jnp.cos(chi)) * lax.rsqrt(noise)


def mm(a, b):
    return jnp.dot(a, b, preferred_element_type=jnp.float32)


def general(micrograph, bank, orient_index, noise_power, defocus):
    slab, ncols = micrograph.shape
    n_rows = lax.axis_size("rows")
    nrows = slab * n_rows
    row_pos = lax.axis_index("rows")
    lcos, lsin = tables(nrows, nrows, nrows)
    ccos, csin = tables(ncols, ncols, ncols)
    piece = lax.all_gather(micrograph, "rows", axis=0, tiled=True)
    part_re = mm(piece, ccos.T).astype(jnp.bfloat16)
    part_im = (-mm(piece, csin.T)).astype(jnp.bfloat16)
    new_re = mm(lcos, part_re) + mm(lsin, part_im)
    new_im = mm(lcos, part_im) - mm(lsin, part_re)
    chosen = jnp.take(bank, orient_index, axis=0)
    mine = lax.all_to_all(chosen, "rows", split_axis=0, concat_axis=1, tiled=True)
    filt = spectral_filter(
        lax.iota(jnp.int32, nrows),
        lax.iota(jnp.int32, ncols),
        nrows,
        ncols,
        defocus[0],
        noise_power,
    )
    scale = 1.0 / (nrows * ncols)
    tcos = ccos.T
    tsin = csin.T

    def correlate(carry, proj):
        tmp_re = mm(proj, tcos).astype(jnp.bfloat16)
        tmp_im = (-mm(proj, tsin)).astype(jnp.bfloat16)
        proj_re = mm(lcos, tmp_re) + mm(lsin, tmp_im)
        proj_im = mm(lcos, tmp_im) - mm(lsin, tmp_re)
        cross_re = (filt * (new_re * proj_re + new_im * proj_im)).astype(jnp.bfloat16)
        cross_im = (filt * (new_im * proj_re - new_re * proj_im)).astype(jnp.bfloat16)
        half_re = (mm(lcos, cross_re) - mm(lsin, cross_im)).astype(jnp.bfloat16)
        half_im = (mm(lcos, cross_im) + mm(lsin, cross_re)).astype(jnp.bfloat16)
        corr = (mm(half_re, ccos) - mm(half_im, csin)) * scale
        best_now, sum_now, square_now = carry
        return ((jnp.maximum(best_now, corr), sum_now + corr, square_now + corr * corr), None)

    start = (
        jnp.full((nrows, ncols), -jnp.inf, jnp.float32),
        jnp.zeros((nrows, ncols), jnp.float32),
        jnp.zeros((nrows, ncols), jnp.float32),
    )
    (best, summed, squared), _ = lax.scan(correlate, start, mine)
    width = ncols // lax.axis_size("orient")
    best = lax.pmax(best, ("orient", "rows"))
    summed, squared = lax.psum((summed, squared), ("orient", "rows"))
    first_col = lax.axis_index("orient") * width
    first_row = row_pos * slab

    def block(field):
        picked = lax.dynamic_slice_in_dim(field, first_row, slab, 0)
        return lax.dynamic_slice_in_dim(picked, first_col, width, 1)

    peak = block(best)
    total = block(summed)
    squares = block(squared)
    return (peak, total, squares)

MESH = pl.DeviceIdType.MESH


def wide_table(count):
    index = np.arange(count)
    phase = (index[:, None] * index[None, :] % count).astype(np.float32) * np.float32(2.0 * math.pi / count)
    cos = np.cos(phase)
    sin = np.sin(phase)
    return np.concatenate([sin, cos, -sin], axis=1).astype(jnp.bfloat16)


def dot(a, b):
    return jnp.dot(a, b, preferred_element_type=jnp.float32)


def kernel(n, m, size, defocus, index, mic_hbm, bank_hbm, noise_hbm, table_hbm, peak, total, squares,
           bank, chosen, mic, noise, table, mics, halves, beside, tmp_mic, tmp, spec_re, spec_im, proj_re, proj_im, cross, half, stage, inbox, part,
           local_sem, near, out_send, out_recv):
    row = lax.axis_index("rows")
    col = lax.axis_index("orient")
    slab = size // n
    width = size // m
    me = row * 2 + lax.rem(col, 2)
    grp = lax.axis_index("grp")
    over = row + 2 - 4 * (row // 2)
    mate = row + 1 - 2 * lax.rem(row, 2)
    corner = mate + 2 - 4 * (mate // 2)
    piece = slab // 2
    barrier = pltpu.get_barrier_semaphore()
    low = 2 * (col // 2)
    far = 2 - low
    for a in range(n):
        for b in range(2):
            if a or b:
                peer = {"rows": lax.rem(row + a, n), "orient": low + lax.rem(col + b, 2)}
                pl.semaphore_signal(barrier, inc=1, device_id=peer, device_id_type=MESH)
    twin = {"orient": far + lax.rem(col, 2)}
    pl.semaphore_signal(barrier, inc=1, device_id=twin, device_id_type=MESH)
    pl.semaphore_signal(barrier, inc=1, device_id={"grp": 1 - grp}, device_id_type=MESH)
    mic_in = pltpu.make_async_copy(mic_hbm, mic, local_sem.at[0])
    table_in = pltpu.make_async_copy(table_hbm, table, local_sem.at[1])
    noise_in = pltpu.make_async_copy(noise_hbm, noise, local_sem.at[2])
    bank_in = pltpu.make_async_copy(bank_hbm, bank, local_sem.at[3])
    bank_in.start()
    mic_in.start()
    table_in.start()
    noise_in.start()
    bank_in.wait()
    for d in range(n):
        chosen[d] = bank[index[d]]
    mic_in.wait()
    pl.semaphore_wait(barrier, 2 * n + 1)

    def remote(src, dst, sems, at, to):
        return pltpu.make_async_remote_copy(
            src_ref=src, dst_ref=dst, send_sem=sems.at[0, at], recv_sem=sems.at[1, at],
            device_id=to, device_id_type=MESH)

    bank_over = remote(chosen.at[over, pl.ds(grp * piece, piece)], halves.at[0, grp], near, 0, {"rows": over})
    bank_corner = remote(chosen.at[corner, pl.ds(grp * piece, piece)], halves.at[1, grp], near, 1, {"rows": corner})
    bank_mate = remote(chosen.at[mate], beside.at[0], near, 2, {"rows": mate})
    mic_over = remote(mic, mics.at[0], near, 3, {"rows": over})
    mic_mate = remote(mic, mics.at[1], near, 4, {"rows": mate})
    mic_pass = remote(mics.at[0], mics.at[2], near, 5, {"rows": mate})
    pass_over = remote(halves.at[0, grp], halves.at[0, grp], near, 6, {"grp": 1 - grp})
    pass_corner = remote(halves.at[1, grp], halves.at[1, grp], near, 7, {"grp": 1 - grp})
    bank_over.start()
    bank_corner.start()
    mic_over.start()
    mic_mate.start()
    bank_mate.start()

    def row_dft(into, block, source):
        at = pl.multiple_of(source * slab, slab)
        both = dot(block, table[:, 0:2 * size]).astype(jnp.bfloat16)
        into[pl.ds(at, slab), :] = both[:, size:]
        into[pl.ds(pl.multiple_of(size + source * slab, slab), slab), :] = both[:, :size]

    table_in.wait()
    row_dft(tmp_mic, mic[...], row)
    row_dft(tmp, chosen[row], row)
    bank_over.wait_recv()
    pass_over.start()
    mic_mate.wait_recv()
    row_dft(tmp_mic, mics[1], mate)
    bank_corner.wait_recv()
    pass_corner.start()
    bank_mate.wait_recv()
    row_dft(tmp, beside[0], mate)
    noise_in.wait()

    def freq_angle(shape, dim):
        k = lax.broadcasted_iota(jnp.int32, shape, dim)
        f = jnp.where(k < size // 2, k, k - size).astype(jnp.float32) / size
        return math.pi * defocus[0] * f * f

    step = 256
    across = freq_angle((8, size), 1)
    sin_x = jnp.sin(across)[0:1]
    cos_x = jnp.cos(across)[0:1]
    left_x = -(0.9975 * cos_x - 0.07 * sin_x)
    right_x = -(0.9975 * sin_x + 0.07 * cos_x)
    down = freq_angle((size, 128), 0)
    sin_y = jnp.sin(down)[:, 0:1]
    cos_y = jnp.cos(down)[:, 0:1]
    for g in range(size // step):
        rows_g = slice(g * step, (g + 1) * step)
        noise[rows_g, :] = (sin_y[rows_g] * left_x + cos_y[rows_g] * right_x) * lax.rsqrt(noise[rows_g, :])
    home = (row // 2) * 2 * slab
    away = (1 - row // 2) * 2 * slab

    def rows_at(first):
        return pl.ds(pl.multiple_of(first, 2 * slab), 2 * slab)

    def partial_re(rows_g, first):
        return dot(table[rows_g, rows_at(size + first)], tmp_mic[rows_at(first), :]) + dot(
            table[rows_g, rows_at(2 * size + first)], tmp_mic[rows_at(size + first), :])

    def partial_im(rows_g, first):
        return dot(table[rows_g, rows_at(first)], tmp_mic[rows_at(first), :]) + dot(
            table[rows_g, rows_at(size + first)], tmp_mic[rows_at(size + first), :])

    for g in range(size // step):
        rows_g = slice(g * step, (g + 1) * step)
        spec_re[rows_g, :] = partial_re(rows_g, home)
        spec_im[rows_g, :] = partial_im(rows_g, home)
    pass_over.wait_recv()
    row_dft(tmp, halves[0].reshape(slab, size), over)
    mic_over.wait_recv()
    mic_pass.start()
    pass_corner.wait_recv()
    row_dft(tmp, halves[1].reshape(slab, size), corner)
    row_dft(tmp_mic, mics[0], over)
    for g in range(size // step):
        rows_g = slice(g * step, (g + 1) * step)
        proj_re[rows_g, :] = noise[rows_g, :] * dot(table[rows_g, size:], tmp[...])
        proj_im[rows_g, :] = noise[rows_g, :] * dot(table[rows_g, :2 * size], tmp[...])
    mic_pass.wait_recv()
    row_dft(tmp_mic, mics[2], corner)
    for g in range(size // step):
        rows_g = slice(g * step, (g + 1) * step)
        s_re = spec_re[rows_g, :] + partial_re(rows_g, away)
        s_im = spec_im[rows_g, :] + partial_im(rows_g, away)
        p_re = proj_re[rows_g, :]
        p_im = proj_im[rows_g, :]
        cross[rows_g, :] = (s_re * p_re + s_im * p_im).astype(jnp.bfloat16)
        cross[size + g * step:size + (g + 1) * step, :] = (s_re * p_im - s_im * p_re).astype(jnp.bfloat16)

    def out_copy(kind, a, b, slot):
        peer = a * 2 + b
        return pltpu.make_async_remote_copy(
            src_ref=stage.at[kind, peer], dst_ref=inbox.at[kind, slot],
            send_sem=out_send.at[kind, peer], recv_sem=out_recv.at[kind, slot],
            device_id={"rows": a, "orient": low + b}, device_id_type=MESH)

    scale = 1.0 / (size * size)
    pairs = n // 2
    side = lax.rem(col, 2)

    def send_blocks(kind, t):
        g = lax.rem(row // 2 + t, pairs)
        begin = (far if kind == 0 else low) * width
        cos_at = pl.ds(pl.multiple_of(size + begin, 2 * width), 2 * width)
        sin_at = pl.ds(pl.multiple_of(2 * size + begin, 2 * width), 2 * width)
        corr = (dot(half[t - 1, :, :size], table[:, cos_at]) + dot(half[t - 1, :, size:], table[:, sin_at])) * scale
        corr = corr.astype(jnp.bfloat16)
        for i in range(2):
            for b in range(2):
                stage[kind, (g * 2 + i) * 2 + b] = corr[i * slab:(i + 1) * slab, b * width:(b + 1) * width]
        for i in range(2):
            a = g * 2 + lax.rem(row + 1 + i, 2)
            for s in (1, 0):
                if t == pairs and i == 1 and s == 0:
                    continue
                out_copy(kind, a, lax.rem(side + s, 2), me).start()

    for t in range(1, pairs + 1):
        at = pl.ds(pl.multiple_of(lax.rem(row // 2 + t, pairs) * 2 * slab, 2 * slab), 2 * slab)
        half[t - 1, :, :size] = dot(table[at, size:], cross[...]).astype(jnp.bfloat16)
        half[t - 1, :, size:] = dot(table[at, :2 * size], cross[...]).astype(jnp.bfloat16)
        send_blocks(0, t)
    for t in range(1, pairs + 1):
        send_blocks(1, t)

    def combine(kind):
        best = summed = stage[kind, me].astype(jnp.float32)
        squared = best * best
        for a in range(n):
            for b in range(2):
                if a or b:
                    ra = lax.rem(row + n - a, n)
                    rb = lax.rem(side + b, 2)
                    source = ra * 2 + rb
                    out_copy(kind, ra, rb, source).wait_recv()
                    value = inbox[kind, source].astype(jnp.float32)
                    best = jnp.maximum(best, value)
                    summed = summed + value
                    squared = squared + value * value
        return best, summed, squared

    best, summed, squared = combine(0)
    part[0, 0] = best.astype(jnp.bfloat16)
    part[0, 1] = summed.astype(jnp.bfloat16)
    part[0, 2] = squared.astype(jnp.bfloat16)
    part_copy = remote(part.at[0], part.at[1], near, 8, twin)
    part_copy.start()
    best, summed, squared = combine(1)
    part_copy.wait_recv()
    best = jnp.maximum(best, part[1, 0].astype(jnp.float32))
    summed = summed + part[1, 1].astype(jnp.float32)
    squared = squared + part[1, 2].astype(jnp.float32)
    peak[...] = best
    total[...] = summed
    squares[...] = squared
    for copy in (bank_over, bank_corner, bank_mate, mic_over, mic_mate, mic_pass, pass_over, pass_corner):
        copy.wait_send()
    part_copy.wait_send()
    for kind in range(2):
        for a in range(n):
            for b in range(2):
                if a or b:
                    out_copy(kind, lax.rem(row + a, n), lax.rem(side + b, 2), me).wait_send()


def write_out(peak_in, total_in, squares_in, peak, total, squares, held, sems):
    reads = [pltpu.make_async_copy(r, held.at[i], sems.at[0, i]) for i, r in enumerate((peak_in, total_in, squares_in))]
    writes = [pltpu.make_async_copy(held.at[i], w, sems.at[1, i]) for i, w in enumerate((peak, total, squares))]
    for copy in reads:
        copy.start()
    for read, write in zip(reads, writes):
        read.wait()
        write.start()
    for copy in writes:
        copy.wait()


def local(micrograph, bank, orient_index, noise_power, defocus):
    slab, size = micrograph.shape
    n = lax.axis_size("rows")
    m = lax.axis_size("orient")
    fits = size == slab * n and n == 4 and m == 4 and lax.axis_size("grp") == 2 and slab % 128 == 0 and (size // m) % 128 == 0 and size % 256 == 0
    if not (fits and orient_index.shape[0] == n and bank.shape[0] <= 64):
        return general(micrograph, bank, orient_index, noise_power, defocus)
    table = jnp.asarray(wide_table(size))
    width = size // m
    out = jax.ShapeDtypeStruct((slab, width), jnp.float32)
    vmem = pl.BlockSpec(memory_space=pltpu.VMEM)
    hbm = pl.BlockSpec(memory_space=pl.ANY)
    smem = pl.BlockSpec(memory_space=pltpu.SMEM)
    bf16 = jnp.bfloat16
    dma = pltpu.SemaphoreType.DMA
    maps = pl.pallas_call(
        functools.partial(kernel, n, m, size),
        out_shape=(out, out, out),
        in_specs=[smem, smem, hbm, hbm, hbm, hbm],
        out_specs=(vmem, vmem, vmem),
        scratch_shapes=[
            pltpu.VMEM(bank.shape, bf16),
            pltpu.VMEM((n, slab, size), bf16),
            pltpu.VMEM((slab, size), bf16),
            pltpu.VMEM((size, size), jnp.float32),
            pltpu.VMEM((size, 3 * size), bf16),
            pltpu.VMEM((3, slab, size), bf16),
            pltpu.VMEM((2, 2, slab // 2, size), bf16),
            pltpu.VMEM((1, slab, size), bf16),
            pltpu.VMEM((2 * size, size), bf16),
            pltpu.VMEM((2 * size, size), bf16),
            pltpu.VMEM((size, size), jnp.float32),
            pltpu.VMEM((size, size), jnp.float32),
            pltpu.VMEM((size, size), jnp.float32),
            pltpu.VMEM((size, size), jnp.float32),
            pltpu.VMEM((2 * size, size), bf16),
            pltpu.VMEM((n // 2, 2 * slab, 2 * size), bf16),
            pltpu.VMEM((2, 2 * n, slab, width), bf16),
            pltpu.VMEM((2, 2 * n, slab, width), bf16),
            pltpu.VMEM((2, 3, slab, width), bf16),
            dma((4,)), dma((2, 9)), dma((2, 2 * n)), dma((2, 2 * n)),
        ],
        compiler_params=pltpu.CompilerParams(collective_id=0, has_side_effects=True, vmem_limit_bytes=60 * 1024 * 1024),
        name="correlate",
    )(defocus, orient_index, micrograph, bank, noise_power, table)
    return pl.pallas_call(
        write_out,
        out_shape=(out, out, out),
        in_specs=[hbm] * 3,
        out_specs=(hbm, hbm, hbm),
        scratch_shapes=[pltpu.VMEM((3, slab, width), jnp.float32), dma((2, 3))],
        name="write_out",
    )(*maps)


def solution(mesh):
    in_specs = (
        P(("grp", "rows"), None),
        P(None, "rows", None),
        P("orient"),
        P("grp", None),
        P("grp"),
    )
    out_specs = (
        P(("grp", "rows"), "orient"),
        P(("grp", "rows"), "orient"),
        P(("grp", "rows"), "orient"),
    )
    return jax.shard_map(local, mesh=mesh, in_specs=in_specs, out_specs=out_specs, check_vma=False)
```
